256 devices in a mesh: outer: 64 (over x_hi, z, y), inner: 4 (over x_lo, core).
Axes of the slice: x: 4 (x_hi: 2, x_lo: 2; x = x_hi * 2 + x_lo), y: 4, z: 8, core: 2. Of those that a mesh axis runs over, the one named last changes fastest.
Arguments:
- queries: bfloat16 [65536, 1536], P(('outer', 'inner')), may hold values from -8 to 8
- key_rows: bfloat16 [65536, 1536], P(('outer', 'inner')), may hold values from -8 to 8
- value_rows: bfloat16 [65536, 1536], P(('outer', 'inner')), may hold values from -6 to 6
- upstream: bfloat16 [65536, 1536], P(('outer', 'inner')), may hold values from -6 to 6
- short_offsets: int32 [16], replicated, may hold values from 0 to 1
- global_offsets: int32 [16], replicated, may hold values from 0 to 127
Outputs:
- grad_queries: bfloat16 [65536, 1536], P(('outer', 'inner'))
- grad_keys: bfloat16 [65536, 1536], P(('outer', 'inner'))
- grad_values: bfloat16 [65536, 1536], P(('outer', 'inner'))
The draws below stay inside these ranges and needn't reach their ends.
All inputs are finite; a program needn't handle non-finite values.
Results may differ from the reference program's by a relative error of at most 0.006.
The reference program's roundings to bfloat16 on the way count: a program that leaves them out, or rounds other values in their place, can miss the bound.
Values may be sent and summed in bfloat16 or wider, within the bound.
No kernel may reach another device: no remote copies, remote signals or barrier semaphores. Data moves between devices by JAX's collectives and lax.ppermute only.
A program may use at most 128 MiB of HBM per device.

```python
import jax
import jax.numpy as jnp
from jax import lax

H = 16
HD = 96
D = 1536
KEEP_B = 512
TOKENS = 65536
SEG = 1024
RATE_A = 2
RATE_B = 128
N_OUTER = 64


def drawn_rows(key, salt):
    base = jax.random.normal(jax.random.fold_in(key, salt), (TOKENS, D), jnp.float32)
    rows = jnp.clip(base, -6.0, 6.0)
    return rows.astype(jnp.bfloat16)


def draw_queries(key, part):
    return drawn_rows(key, 1)


def draw_key_rows(key, part):
    return drawn_rows(key, 2)


def with_ends(entries, own_key, smallest, top_value):
    longest = entries.shape.index(max(entries.shape))
    spots = []
    for shift in (0, 1):
        where = [jax.random.randint(jax.random.fold_in(own_key, axis), (), 0, length) for axis, length in enumerate(entries.shape)]
        where[longest] = (where[longest] + shift) % entries.shape[longest]
        spots.append(tuple(where))
    return entries.at[spots[0]].set(smallest).at[spots[1]].set(top_value)


def steps_of(key, extent, shards, low, largest):
    gain, own = 1.0, jax.random.fold_in(key, 6)
    for dim, shards_of in shards:
        draws = jnp.exp(jax.random.uniform(jax.random.fold_in(own, dim), (shards_of,), jnp.float32, low / len(shards), largest / len(shards)))
        gain = gain * jnp.repeat(draws, extent[dim] // shards_of).reshape([-1 if axis == dim else 1 for axis in range(len(extent))])
    return gain


def centred(rng, shape, scale, reach, pieces=(), kind=jnp.bfloat16):
    result = jax.random.normal(rng, shape, jnp.float32) * scale
    if len(pieces) > 0:
        result = steps_of(rng, shape, pieces, -0.22, 0.18) * result
    return jnp.clip(result, min=-reach, max=reach).astype(kind)


def setup_inputs(seed: int = 0) -> dict:
    splits = jax.random.split(jax.random.key(seed), 7)
    queries = draw_queries(jax.random.fold_in(splits[6], 71), 0)
    key_rows = draw_key_rows(jax.random.fold_in(splits[6], 71), 0)
    value_rows = centred(splits[2], (TOKENS, D), 1.0, 6.0, ((0, 256),))
    upstream = centred(splits[3], (TOKENS, D), 1.0, 6.0, ((0, 256),))
    short_offsets = with_ends(jax.random.randint(splits[4], (H,), 0, RATE_A), jax.random.fold_in(splits[4], 1), 0, RATE_A - 1).astype(jnp.int32)
    global_offsets = with_ends(jax.random.randint(splits[5], (H,), 0, RATE_B), jax.random.fold_in(splits[5], 1), 0, RATE_B - 1).astype(jnp.int32)
    return dict(queries=queries, key_rows=key_rows, value_rows=value_rows, upstream=upstream, short_offsets=short_offsets, global_offsets=global_offsets)


def pick_rows(block, offsets, stride):
    count = block.shape[0] // stride
    shaped = block.reshape(count, stride, H, HD)
    onehot = (jnp.arange(stride, dtype=jnp.int32)[:, None] == offsets[None, :]).astype(block.dtype)
    return jnp.sum(shaped * onehot[None, :, :, None], axis=1)


def put_rows(grads, offsets, stride):
    onehot = (jnp.arange(stride, dtype=jnp.int32)[:, None] == offsets[None, :]).astype(jnp.float32)
    spread = grads[:, None, :, :] * onehot[None, :, :, None]
    return spread.reshape(grads.shape[0] * stride, H * HD)


def attend_back(query_part, key_part, value_part, grad_part):
    softmax_scale = HD ** -0.5
    qf = query_part.astype(jnp.float32)
    kf = key_part.astype(jnp.float32)
    vf = value_part.astype(jnp.float32)
    gf = grad_part.astype(jnp.float32)
    scores = jnp.einsum('qhd,khd->hqk', qf, kf) * softmax_scale
    row_max = jnp.max(scores, axis=-1, keepdims=True)
    weights = jnp.exp(scores - row_max)
    probs = weights / jnp.sum(weights, axis=-1, keepdims=True)
    probs_low = probs.astype(jnp.bfloat16).astype(jnp.float32)
    output = jnp.einsum('hqk,khd->qhd', probs_low, vf)
    delta = jnp.sum(gf * output, axis=-1)
    dprobs = jnp.einsum('qhd,khd->hqk', gf, vf)
    dscores = (probs * (dprobs - jnp.transpose(delta)[:, :, None])).astype(jnp.bfloat16).astype(jnp.float32)
    grad_q = jnp.einsum('hqk,khd->qhd', dscores, kf) * softmax_scale
    grad_k = jnp.einsum('hqk,qhd->khd', dscores, qf) * softmax_scale
    grad_v = jnp.einsum('hqk,qhd->khd', probs_low, gf)
    return grad_q, grad_k, grad_v


def reference(queries, key_rows, value_rows, upstream, short_offsets, global_offsets):
    far = [pick_rows(member, global_offsets, RATE_B) for member in (queries, key_rows, value_rows, upstream)]
    far_grads = attend_back(far[0], far[1], far[2], far[3])
    per_seg = KEEP_B // N_OUTER
    far_split = [member.reshape(N_OUTER, per_seg, H, HD) for member in far_grads]
    blocks = [member.reshape(N_OUTER, SEG, D) for member in (queries, key_rows, value_rows, upstream)]

    def segment(pack):
        near = [pick_rows(pack[index], short_offsets, RATE_A) for index in range(4)]
        near_grads = attend_back(near[0], near[1], near[2], near[3])
        results = []
        for index in range(3):
            total = put_rows(near_grads[index], short_offsets, RATE_A) + put_rows(pack[4 + index], global_offsets, RATE_B)
            results.append(total.astype(jnp.bfloat16))
        return results[0], results[1], results[2]

    out_q, out_k, out_v = lax.map(segment, (blocks[0], blocks[1], blocks[2], blocks[3], far_split[0], far_split[1], far_split[2]))
    return out_q.reshape(TOKENS, D), out_k.reshape(TOKENS, D), out_v.reshape(TOKENS, D)
```

```python
import jax
import jax.numpy as jnp
from jax import lax
from jax.experimental import pallas as pl
from jax.experimental.pallas import tpu as pltpu
from jax.sharding import Mesh
from jax.sharding import PartitionSpec as P


H = 16
HD = 96
D = 1536
TOK = 256
NEAR = 128
FAR_STRIDE = 128
GROUP = 4
LANES = GROUP * HD
INNER = 4
SCALE = HD ** -0.5
LOG2E = 1.4426950408889634

ALL_AXES = ("xh", "zh", "zl", "y", "xl", "c")
SIZES = (2, 2, 4, 4, 2, 2)
PAIR = ("xl", "c")
CORE_GROUPS = [[2 * chip + core for chip in range(127, -1, -1)] for core in range(2)]
HEAD_GROUPS = [[64 * r + 4 * h + rest for h in range(15, -1, -1)] for r in range(4) for rest in range(4)]


def nn(a, b):
    return lax.dot_general(a, b, (((1,), (0,)), ((), ())), preferred_element_type=jnp.float32)


def nt(a, b):
    return lax.dot_general(a, b, (((1,), (1,)), ((), ())), preferred_element_type=jnp.float32)


def tn(a, b):
    return lax.dot_general(a, b, (((0,), (0,)), ((), ())), preferred_element_type=jnp.float32)


def lane_of_heads(values, shape):
    lane = lax.broadcasted_iota(jnp.int32, shape, len(shape) - 1)
    spread = jnp.full(shape, values[-1], jnp.int32)
    for hl in range(len(values) - 2, -1, -1):
        spread = jnp.where(lane < (hl + 1) * HD, values[hl], spread)
    return spread


RESIDENT = pl.BlockSpec(memory_space=pltpu.VMEM)


def resident(shape, dtype):
    return pltpu.VMEM(shape, dtype)


GRANT = pltpu.CompilerParams(vmem_limit_bytes=20 * 2**20)


def in_hbm(xs):
    return [pltpu.with_memory_space_constraint(x, pltpu.HBM) for x in xs]


def kept(xs):
    return [pltpu.with_memory_space_constraint(x, pltpu.VMEM) for x in xs]


SCALARS = pl.BlockSpec(memory_space=pltpu.SMEM)
REMAIN = pl.BlockSpec(memory_space=pltpu.HBM)


def pick_kernel(so, go, q_ref, k_ref, v_ref, g_ref, *outs):
    near_refs, (far_ref, blocks, near, selector, rows, low, in_sems, sems) = outs[:INNER], outs[INNER:]
    loads = []
    for t, ref in enumerate((q_ref, k_ref, v_ref, g_ref)):
        for half in range(2):
            part = pl.ds(half * NEAR, NEAR)
            loads.append(pltpu.make_async_copy(ref.at[part], blocks.at[t, part], in_sems.at[2 * t + half]))
    for load in loads:
        load.start()
    me = lax.axis_index(PAIR)
    row = lax.broadcasted_iota(jnp.int32, (2 * NEAR, TOK), 0)
    col = lax.broadcasted_iota(jnp.int32, (2 * NEAR, TOK), 1)
    target = jnp.where(row < NEAR, 2 * row, 2 * (row - NEAR) + 1)
    selector[: 2 * NEAR, :] = (col == target).astype(jnp.bfloat16)
    frow = lax.broadcasted_iota(jnp.int32, (2 * H, TOK), 0)
    fcol = lax.broadcasted_iota(jnp.int32, (2 * H, TOK), 1)
    ftarget = jnp.zeros((2 * H, TOK), jnp.int32)
    for h in range(H):
        ftarget = jnp.where(frow >= 2 * h, go[h], ftarget)
    ftarget = ftarget + FAR_STRIDE * (frow & 1)
    selector[2 * NEAR :, :] = (fcol == ftarget).astype(jnp.bfloat16)
    fars = []
    for t in range(4):
        loads[2 * t].wait()
        loads[2 * t + 1].wait()
        for g in range(INNER):
            lanes = slice(g * LANES, (g + 1) * LANES)
            odd = lane_of_heads([so[g * GROUP + hl] for hl in range(GROUP)], (1, LANES)) == 1
            both = nn(selector[...], blocks[t, :, lanes])
            near[t, :, lanes] = jnp.where(odd, both[NEAR : 2 * NEAR], both[:NEAR]).astype(jnp.bfloat16)
            fars.append(both[2 * NEAR + 8 * g : 2 * NEAR + 8 * (g + 1)])
    for h in range(H):
        g, hl = divmod(h, GROUP)
        for j in range(2):
            line = [fars[t * INNER + g][2 * hl + j : 2 * hl + j + 1, hl * HD : (hl + 1) * HD] for t in range(4)]
            line = jnp.concatenate(line, axis=1)
            for xl in range(2):
                rows[2 * (H - 1 - h) + xl, j : j + 1, :] = line
    low[...] = rows[...].astype(jnp.bfloat16)
    copies = [pltpu.make_async_copy(low, far_ref.at[pl.ds(r * 2 * H, 2 * H)], sems.at[r]) for r in range(4)]
    for copy in copies:
        copy.start()
    for m in range(INNER):
        lanes = pl.ds(pl.multiple_of((me ^ m) * LANES, LANES), LANES)
        for t in range(4):
            near_refs[m][:, t * LANES : (t + 1) * LANES] = near[t, :, lanes]
    for copy in copies:
        copy.wait()


def pick(so, go, members):
    return pl.pallas_call(
        pick_kernel,
        in_specs=[SCALARS] * 2 + [REMAIN] * 4,
        out_specs=[RESIDENT] * INNER + [REMAIN],
        scratch_shapes=[
            pltpu.VMEM((4, TOK, D), jnp.bfloat16),
            pltpu.VMEM((4, NEAR, D), jnp.bfloat16),
            pltpu.VMEM((2 * NEAR + 2 * H, TOK), jnp.bfloat16),
            pltpu.VMEM((2 * H, 2, LANES), jnp.float32),
            pltpu.VMEM((2 * H, 2, LANES), jnp.bfloat16),
            pltpu.SemaphoreType.DMA((8,)),
            pltpu.SemaphoreType.DMA((4,)),
        ],
        out_shape=[resident((NEAR, 4 * LANES), jnp.bfloat16)] * INNER + [pltpu.HBM((128, 2, LANES), jnp.bfloat16)],
        compiler_params=GRANT,
        name="pick",
    )(*in_hbm([so, go, *members]))


def attend(q, k, v, g):
    scores = nt(k, q)
    top = jnp.max(scores, axis=0, keepdims=True)
    weights = jnp.exp2((scores - top) * (SCALE * LOG2E))
    probs = weights * (1.0 / jnp.sum(weights, axis=0, keepdims=True))
    low = probs.astype(jnp.bfloat16)
    dprobs = nt(v, g)
    delta = jnp.sum(low.astype(jnp.float32) * dprobs, axis=0, keepdims=True)
    dscores = (probs * (dprobs - delta)).astype(jnp.bfloat16)
    return tn(k, dscores).T * SCALE, nn(dscores, q) * SCALE, nn(low, g)


def near_kernel(*refs):
    ins, outs = refs[:INNER], refs[INNER:]
    for hl in range(GROUP):
        parts = []
        for t in range(4):
            lo = t * LANES + hl * HD
            parts.append(jnp.concatenate([ref[:, lo : lo + HD] for ref in ins], axis=0))
        for a, grad in enumerate(attend(*parts)):
            low = grad.astype(jnp.bfloat16)
            lo = a * LANES + hl * HD
            for m, out in enumerate(outs):
                out[:, lo : lo + HD] = low[m * NEAR : (m + 1) * NEAR]


def near_back(blocks):
    return pl.pallas_call(
        near_kernel,
        in_specs=[RESIDENT] * INNER,
        out_specs=[RESIDENT] * INNER,
        out_shape=[resident((NEAR, 3 * LANES), jnp.bfloat16)] * INNER,
        compiler_params=GRANT,
        name="near_back",
    )(*kept(blocks))


def far_kernel(own_ref, other_ref, out_ref, grads_ref):
    rows = jnp.concatenate([ref[...].reshape(256, LANES) for ref in (own_ref, other_ref)], axis=0)
    grads = attend(*[rows[:, t * HD : (t + 1) * HD] for t in range(4)])
    first = (3 - lax.axis_index(("xh", "zh"))) * 64 + 2 - 2 * lax.axis_index("xl")
    for a in range(3):
        grads_ref[a] = grads[a]
    for a in range(3):
        for j in range(2):
            out_ref[:, 2 * a + j, :] = grads_ref[a, pl.ds(first + j, 16, stride=4), :]
    out_ref[:, 6, :] = jnp.zeros((16, HD), jnp.float32)
    out_ref[:, 7, :] = jnp.zeros((16, HD), jnp.float32)


def far_back(halves):
    return pl.pallas_call(
        far_kernel,
        in_specs=[RESIDENT] * 2,
        out_specs=RESIDENT,
        scratch_shapes=[pltpu.VMEM((3, 512, HD), jnp.float32)],
        out_shape=resident((16, 8, HD), jnp.float32),
        compiler_params=GRANT,
        name="far_back",
    )(*kept(halves))


def spread_kernel(so, *refs):
    near_refs, outs = refs[:INNER], refs[INNER:]
    me = lax.axis_index(PAIR)
    row = lax.broadcasted_iota(jnp.int32, (TOK, 2 * NEAR), 0)
    col = lax.broadcasted_iota(jnp.int32, (TOK, 2 * NEAR), 1)
    target = jnp.where(col < NEAR, 2 * col, 2 * (col - NEAR) + 1)
    spread = (row == target).astype(jnp.bfloat16)
    for m in range(INNER):
        group = me ^ m
        odd = lane_of_heads([so[group * GROUP + hl] for hl in range(GROUP)], (1, LANES)) == 1
        lanes = pl.ds(pl.multiple_of(group * LANES, LANES), LANES)
        for a, out in enumerate(outs):
            rows = near_refs[m][:, a * LANES : (a + 1) * LANES]
            zero = jnp.zeros_like(rows)
            stacked = jnp.concatenate([jnp.where(odd, zero, rows), jnp.where(odd, rows, zero)], axis=0)
            out[:, lanes] = nn(spread, stacked).astype(jnp.bfloat16)


def spread_rows(so, near):
    return pl.pallas_call(
        spread_kernel,
        in_specs=[SCALARS] + [RESIDENT] * INNER,
        out_specs=[RESIDENT] * 3,
        out_shape=[resident((TOK, D), jnp.bfloat16)] * 3,
        compiler_params=GRANT,
        name="spread",
    )(*in_hbm([so]), *kept(near))


def finish_kernel(go, n0, n1, n2, far_ref, *rest):
    outs, (stage, sems) = rest[:3], rest[3:]
    stores = []
    for a, (near, out) in enumerate(zip((n0, n1, n2), outs)):
        for j in range(2):
            part = slice(j * FAR_STRIDE, (j + 1) * FAR_STRIDE)
            for g in range(INNER):
                lanes = slice(g * LANES, (g + 1) * LANES)
                spot = lane_of_heads([go[g * GROUP + hl] for hl in range(GROUP)], (1, LANES))
                here = lax.broadcasted_iota(jnp.int32, (FAR_STRIDE, LANES), 0) == spot
                line = jnp.concatenate(
                    [far_ref[H - 1 - g * GROUP - hl, 2 * a + j : 2 * a + j + 1, :] for hl in range(GROUP)], axis=1
                )
                total = near[part, lanes].astype(jnp.float32) + jnp.where(here, line, 0.0)
                stage[a, part, lanes] = total.astype(jnp.bfloat16)
            store = pltpu.make_async_copy(stage.at[a, part], out.at[part], sems.at[2 * a + j])
            store.start()
            stores.append(store)
    for store in stores:
        store.wait()


def finish(go, near, far):
    return pl.pallas_call(
        finish_kernel,
        in_specs=[SCALARS] + [RESIDENT] * 4,
        out_specs=[REMAIN] * 3,
        scratch_shapes=[pltpu.VMEM((3, TOK, D), jnp.bfloat16), pltpu.SemaphoreType.DMA((6,))],
        out_shape=[pltpu.HBM((TOK, D), jnp.bfloat16)] * 3,
        compiler_params=GRANT,
        name="finish",
    )(*in_hbm([go]), *kept([*near, far]))


def swap(x, m):
    return lax.ppermute(x, PAIR, [(i, i ^ m) for i in range(INNER)])


def exchange(blocks):
    out = [blocks[0]]
    for m in range(1, INNER):
        out.append(swap(blocks[m], m))
    return out


def local(queries, key_rows, value_rows, upstream, short_offsets, global_offsets):
    *mine, far_out = pick(short_offsets, global_offsets, (queries, key_rows, value_rows, upstream))
    blocks = exchange(mine)
    far = lax.all_to_all(far_out, ALL_AXES, 0, 0, axis_index_groups=CORE_GROUPS, tiled=True)
    other = lax.ppermute(far, "c", [(0, 1), (1, 0)])
    near = exchange(near_back(blocks))
    far = far_back([far, other])
    far = lax.all_to_all(far, ALL_AXES, 0, 0, axis_index_groups=HEAD_GROUPS, tiled=True)
    return tuple(finish(global_offsets, spread_rows(short_offsets, near), far))


def solution(mesh):
    split = Mesh(mesh.devices.reshape(SIZES), ALL_AXES)
    rows = P(ALL_AXES, None)
    return jax.shard_map(
        local, mesh=split, in_specs=(rows,) * 4 + (P(), P()), out_specs=(rows,) * 3, check_vma=False
    )
```
